32 devices in a mesh: row: 4 (over z), col: 4 (over x, core), tm: 2 (over y).
Axes of the slice: x: 2, y: 2, z: 4, core: 2. Of those that a mesh axis runs over, the one named last changes fastest.
Arguments:
- samples: bfloat16 [1024, 4, 2, 16384], P('row', None, 'tm', 'col'), may hold values from -6 to 6
- whitening: bfloat16 [1024, 1024], replicated, may hold values from -0.1875 to 0.1875
- ridge: float32 [2048], P('col'), may hold values from 2 to 20
- slab_start: int32 [1], replicated, may hold values from 0 to 63
- panels: int32 [4], replicated, may hold values from 0 to 3, as said below
Outputs:
- trailing: float32 [131072, 2048], P(('row', 'tm'), 'col')
- factor: bfloat16 [2, 131072, 512], P(None, ('row', 'tm'))
The draws below stay inside these ranges and needn't reach their ends.
Inputs may be any that keep to these rules, and one draw needn't show every extreme that they name: `panels`: each panel index once.
All inputs are finite; a program needn't handle non-finite values.
Results may differ from the reference program's by a relative error of at most 0.012.
The reference program's roundings to bfloat16 on the way count: a program that leaves them out, or rounds other values in their place, can miss the bound.
Values may be sent and summed in bfloat16 or wider, within the bound.
A program may use at most 256 MiB of HBM per device.

```python
import math
import jax
import jax.numpy as jnp
from jax import lax

K = 131072
S = 1024
PANEL = 512
PANELS = 2
SLAB = 2048
KD = 16384
N_ROW = 4
N_COL = 4
N_TM = 2


def draw_panels(key, part):
    scored = jax.random.fold_in(key, 9173)
    scores = jax.random.randint(scored, (N_COL,), 0, 1 << 20) * N_COL + jnp.arange(N_COL, dtype=jnp.int32)
    return jnp.argsort(scores, stable=True).astype(jnp.int32)


def steps_of(stream_key, dims, cuts, low, largest):
    level, own = 1.0, jax.random.fold_in(stream_key, 6)
    for position, shards_of in cuts:
        steps = jnp.exp(jax.random.uniform(jax.random.fold_in(own, position), (shards_of,), jnp.float32, low / len(cuts), largest / len(cuts)))
        level = level * jnp.repeat(steps, dims[position] // shards_of).reshape([-1 if axis == position else 1 for axis in range(len(dims))])
    return level


def centred(key, shape, spread, bound, split=(), kind=jnp.bfloat16):
    level = steps_of(key, shape, split, -0.22, 0.18) if split else 1.0
    values = jax.random.normal(key, shape, jnp.float32) * spread * level
    return jnp.minimum(jnp.maximum(values, -bound), bound).astype(kind)


def setup_inputs(seed: int = 0) -> dict:
    keys = jax.random.split(jax.random.key(seed), 6)
    samples = centred(keys[0], (S, N_ROW, N_TM, KD), 1.0, 6.0, ((0, 4), (2, 2), (3, 4)))
    whitening = centred(keys[1], (S, S), S ** -0.5, 0.1875)
    ridge = jnp.clip(jnp.exp(math.log(20.0) - 2.3025851 * jax.random.uniform(keys[2], (SLAB,), jnp.float32) ** steps_of(keys[2], (SLAB,), ((0, 4),), -0.2, 0.2)), 2.0, 20.0)
    slab_start = jax.random.randint(keys[3], (1,), 0, K // SLAB).astype(jnp.int32)
    panels = draw_panels(jax.random.fold_in(keys[5], 71), 0)
    return {"samples": samples, "whitening": whitening, "ridge": ridge, "slab_start": slab_start, "panels": panels}


def reference(samples, whitening, ridge, slab_start, panels):
    flat_data = samples.reshape(S, K)
    whitened = jnp.dot(whitening.astype(jnp.float32), flat_data.astype(jnp.float32), preferred_element_type=jnp.float32).astype(jnp.bfloat16)
    slab_first = (slab_start[0] * SLAB).astype(jnp.int32)
    slab_data = lax.dynamic_slice_in_dim(whitened, slab_first, SLAB, 1)
    covariance = lax.dot_general(whitened.astype(jnp.float32), slab_data.astype(jnp.float32), (((0,), (0,)), ((), ())), preferred_element_type=jnp.float32) * (1.0 / math.sqrt(S))
    zero_index = jnp.zeros((), jnp.int32)
    diag_block = lax.dynamic_slice(covariance, (slab_first, zero_index), (SLAB, SLAB)) + jnp.diag(ridge)
    covariance = lax.dynamic_update_slice(covariance, diag_block, (slab_first, zero_index))
    factors = []
    for section in range(PANELS):
        panel_first = (panels[section] * PANEL).astype(jnp.int32)
        pivot_rows = lax.dynamic_slice_in_dim(covariance, slab_first + panel_first, PANEL, 0)
        pivot_diag = lax.dynamic_slice_in_dim(pivot_rows, panel_first, PANEL, 1)
        lower_factor = jnp.linalg.cholesky(pivot_diag)
        panel_columns = lax.dynamic_slice_in_dim(covariance, panel_first, PANEL, 1)
        panel_now = jax.scipy.linalg.solve_triangular(lower_factor, panel_columns.T, lower=True).T.astype(jnp.bfloat16)
        coupling = jax.scipy.linalg.solve_triangular(lower_factor, pivot_rows, lower=True).T.astype(jnp.bfloat16)
        covariance = covariance - lax.dot_general(panel_now.astype(jnp.float32), coupling.astype(jnp.float32), (((1,), (1,)), ((), ())), preferred_element_type=jnp.float32)
        factors.append(panel_now)
    column_panel = jnp.arange(SLAB) // PANEL
    finished = column_panel == panels[0]
    for section in range(1, PANELS):
        finished = finished | (column_panel == panels[section])
    trailing = jnp.where(finished[None, :], jnp.zeros((), covariance.dtype), covariance)
    return (trailing, jnp.stack(factors))
```

```python
import functools
import math
import jax
import jax.numpy as jnp
from jax import lax
from jax.experimental import pallas as pl
from jax.experimental.pallas import tpu as pltpu
from jax.sharding import PartitionSpec as P

NB = 128
SUB = 8
HIGH = lax.Precision.HIGHEST


def block_inverse(a):
    n = NB // SUB
    rows = [a[s * SUB:(s + 1) * SUB, :] for s in range(n)]
    lane = lax.broadcasted_iota(jnp.int32, (SUB, NB), 1)
    sub = lax.broadcasted_iota(jnp.int32, (SUB, NB), 0)
    inv = [jnp.where(lane == sub + s * SUB, 1.0, 0.0).astype(jnp.float32) for s in range(n)]
    for k in range(NB):
        s0, r = divmod(k, SUB)
        row_a = rows[s0][r:r + 1, :]
        row_v = inv[s0][r:r + 1, :]
        scale = 1.0 / row_a[:, k:k + 1]
        row_a_s = row_a * scale
        row_v_s = row_v * scale
        for s in range(s0, n):
            column = jnp.broadcast_to(rows[s][:, k:k + 1], (SUB, NB))
            if s == s0:
                if r == SUB - 1:
                    continue
                column = jnp.where(sub > r, column, 0.0)
            rows[s] = rows[s] - column * row_a_s
            inv[s] = inv[s] - column * row_v_s
    out = []
    for s in range(n):
        d = jnp.sum(jnp.where(lane == sub + s * SUB, rows[s], 0.0), axis=1, keepdims=True)
        out.append(inv[s] / jnp.sqrt(d))
    return jnp.concatenate(out, axis=0)


def inverse_kernel(a_ref, o_ref, work):
    size = a_ref.shape[0]
    work[:, :size] = a_ref[...]
    ri = lax.broadcasted_iota(jnp.int32, (size, size), 0)
    ci = lax.broadcasted_iota(jnp.int32, (size, size), 1)
    work[:, size:] = jnp.where(ri == ci, 1.0, 0.0).astype(jnp.float32)
    row_id = lax.broadcasted_iota(jnp.int32, (size, 1), 0)

    def step(b, carry):
        at = pl.multiple_of(b * NB, NB)
        small = block_inverse(work[pl.ds(at, NB), pl.ds(at, NB)])
        top = jnp.dot(small, work[pl.ds(at, NB), :], preferred_element_type=jnp.float32, precision=HIGH)
        left = jnp.where(row_id >= at + NB, top[:, :size].T, 0.0)
        update = jnp.dot(left, top, preferred_element_type=jnp.float32, precision=HIGH)
        work[...] = work[...] - update
        work[pl.ds(at, NB), :] = top
        return carry

    lax.fori_loop(0, size // NB, step, 0)
    o_ref[...] = work[:, size:]


def lower_inverse(a):
    size = a.shape[0]
    return pl.pallas_call(
        inverse_kernel,
        out_shape=jax.ShapeDtypeStruct((size, size), jnp.float32),
        in_specs=[pl.BlockSpec(memory_space=pltpu.VMEM)],
        out_specs=pl.BlockSpec(memory_space=pltpu.VMEM),
        scratch_shapes=[pltpu.VMEM((size, 2 * size), jnp.float32)],
        compiler_params=pltpu.CompilerParams(vmem_limit_bytes=40 * 2**20),
        name="lower_inverse",
    )(a)


def final_kernel(bm, chunk_base, info, x_ref, m_ref, d0_ref, d1_ref, dn_ref, *rest):
    t_ref, f_ref = rest[-2:]
    width = t_ref.shape[1]
    acc = jnp.dot(x_ref[...], m_ref[...], preferred_element_type=jnp.float32)
    block = chunk_base(pl.program_id(0), pl.program_id(1))
    inside = (block >= info[0]) & (block < info[1])

    @pl.when(inside)
    def _():
        f_ref[0] = (acc[:, :width] + d0_ref[...]).astype(f_ref.dtype)
        f_ref[1] = (acc[:, width:2 * width] + d1_ref[...]).astype(f_ref.dtype)
        t_ref[...] = acc[:, 2 * width:] + dn_ref[...]

    @pl.when(jnp.logical_not(inside))
    def _():
        f_ref[0] = acc[:, :width].astype(f_ref.dtype)
        f_ref[1] = acc[:, width:2 * width].astype(f_ref.dtype)
        t_ref[...] = acc[:, 2 * width:]


def final_chunk(info, x, weights, d0, d1, dn, prior, chunk, chunks, cols, local, width, bm):
    w = local // chunks
    per = w // bm
    rows = cols * local
    depth = x.shape[1]

    def base(c, i):
        return c * (local // bm) + chunk * per + i

    def d_map(c, i, info):
        block = base(c, i)
        inside = (block >= info[0]) & (block < info[1])
        return (jnp.where(inside, block - info[0], 0), 0)

    in_specs = [
        pl.BlockSpec((bm, depth), lambda c, i, info: (c * per + i, 0)),
        pl.BlockSpec((depth, 3 * width), lambda c, i, info: (0, 0)),
        pl.BlockSpec((bm, width), d_map),
        pl.BlockSpec((bm, width), d_map),
        pl.BlockSpec((bm, width), d_map),
    ]
    operands = [info, x, weights, d0, d1, dn]
    aliases = {}
    if prior is not None:
        in_specs += [pl.BlockSpec(memory_space=pl.ANY)] * 2
        operands += list(prior)
        aliases = {6: 0, 7: 1}
    return pl.pallas_call(
        functools.partial(final_kernel, bm, base),
        grid_spec=pltpu.PrefetchScalarGridSpec(
            num_scalar_prefetch=1,
            grid=(cols, per),
            in_specs=in_specs,
            out_specs=[
                pl.BlockSpec((bm, width), lambda c, i, info: (base(c, i), 0)),
                pl.BlockSpec((2, bm, width), lambda c, i, info: (0, base(c, i), 0)),
            ],
        ),
        out_shape=[
            jax.ShapeDtypeStruct((rows, width), jnp.float32),
            jax.ShapeDtypeStruct((2, rows, width), jnp.bfloat16),
        ],
        input_output_aliases=aliases,
        compiler_params=pltpu.CompilerParams(
            vmem_limit_bytes=48 * 2**20, dimension_semantics=("arbitrary", "arbitrary")
        ),
        name="final",
    )(*operands)


def high(a, b, dims):
    return lax.dot_general(a, b, ((dims[:1], dims[1:]), ((), ())), preferred_element_type=jnp.float32, precision=HIGH)


def on_device(samples, whitening, ridge, slab_start, panels):
    times, groups, _, local = samples.shape
    cols = lax.axis_size("col")
    tms = lax.axis_size("tm")
    width = ridge.shape[0]
    slab = width * cols
    kd = local * cols
    depth = whitening.shape[0]
    scale = 1.0 / math.sqrt(depth)
    me_col = lax.axis_index("col")
    me_tm = lax.axis_index("tm")
    me_row = lax.axis_index("row")

    first = slab_start[0] * slab
    group = first // (tms * kd)
    tm_owner = (first % (tms * kd)) // kd
    offset = first % kd

    mine = lax.dynamic_index_in_dim(samples[:, :, 0], group, 1, keepdims=False)
    pieces = []
    for p in range(cols):
        at = offset + p * width
        have = (me_tm == tm_owner) & (me_col == at // local)
        part = lax.dynamic_slice_in_dim(mine, at % local, width, 1)
        pieces.append(jnp.where(have, part, jnp.zeros_like(part)))
    raw = lax.psum(jnp.concatenate(pieces, axis=1), ("tm", "col"))
    raw = lax.all_gather(raw, "row", axis=0, tiled=True)
    ridge_all = lax.all_gather(ridge, "col", axis=0, tiled=True)

    chunks = 4 if local >= 4096 else 2
    w = local // chunks
    gathered = []
    for c in range(chunks):
        moved = lax.all_to_all(samples[:, :, :, c * w:(c + 1) * w], "row", split_axis=1, concat_axis=0, tiled=True)
        moved = moved.reshape(depth, w)
        series = lax.dot_general(
            moved, whitening, (((0,), (1,)), ((), ())), preferred_element_type=jnp.float32
        ).astype(jnp.bfloat16)
        gathered.append(lax.all_gather(series, "col", axis=0, tiled=True))

    sw = jnp.dot(whitening, raw, preferred_element_type=jnp.float32).astype(jnp.bfloat16)
    cut = lambda q: lax.dynamic_slice_in_dim(sw, q * width, width, 1)
    q0, q1 = panels[0], panels[1]
    s0, s1, sj = cut(q0), cut(q1), cut(me_col)
    r0 = lax.dynamic_slice_in_dim(ridge_all, q0 * width, width, 0)
    r1 = lax.dynamic_slice_in_dim(ridge_all, q1 * width, width, 0)
    both = jnp.concatenate([s0, s1], axis=1)
    gram = lax.dot_general(
        both, jnp.concatenate([both, sj], axis=1), (((0,), (0,)), ((), ())), preferred_element_type=jnp.float32
    ) * scale
    own0 = (q0 == me_col).astype(jnp.float32)
    own1 = (q1 == me_col).astype(jnp.float32)
    a00 = gram[:width, :width] + jnp.diag(r0)
    a01 = gram[:width, width:2 * width]
    a0j = gram[:width, 2 * width:] + jnp.diag(r0) * own0
    a11 = gram[width:, width:2 * width] + jnp.diag(r1)
    a1j = gram[width:, 2 * width:] + jnp.diag(r1) * own1
    i0 = lower_inverse(a00)
    c0 = high(i0, jnp.concatenate([a01, a0j], axis=1), (1, 0)).astype(jnp.bfloat16)
    c01, c0j = c0[:, :width], c0[:, width:]
    fix = lax.dot_general(c01, c0, (((0,), (0,)), ((), ())), preferred_element_type=jnp.float32)
    i1 = lower_inverse(a11 - fix[:, :width])
    c1j = high(i1, a1j - fix[:, width:], (1, 0)).astype(jnp.bfloat16)

    zero = jnp.zeros((width, width), jnp.float32)
    e0 = jnp.diag(r0)
    e1 = jnp.diag(r1)
    m0 = high(jnp.concatenate([s0.astype(jnp.float32) * scale, e0], axis=0), i0, (1, 1))
    m0z = jnp.concatenate([m0, zero], axis=0)
    t1 = jnp.concatenate([s1.astype(jnp.float32) * scale, zero, e1], axis=0) - high(
        m0z, c01.astype(jnp.float32), (1, 0))
    m1 = high(t1, i1, (1, 1))
    base = jnp.concatenate([sj.astype(jnp.float32) * scale, zero, zero], axis=0)
    n = base - high(m0z, c0j.astype(jnp.float32), (1, 0)) - high(m1, c1j.astype(jnp.float32), (1, 0))
    finished = (me_col == q0) | (me_col == q1)
    n = jnp.where(finished, 0.0, n)
    weights = jnp.concatenate([m0[:depth], m1[:depth], n[:depth]], axis=1).astype(jnp.bfloat16)

    def spread(rows):
        out = jnp.zeros((slab, width), jnp.float32)
        out = lax.dynamic_update_slice(out, rows[:width], (q0 * width, jnp.zeros((), jnp.int32)))
        return lax.dynamic_update_slice(out, rows[width:], (q1 * width, jnp.zeros((), jnp.int32)))

    d0 = spread(m0z[depth:])
    d1 = spread(m1[depth:])
    own_ridge = jnp.where(finished, 0.0, jnp.diag(ridge))
    dn = spread(n[depth:])
    zi = jnp.zeros((), jnp.int32)
    at = (me_col * width, zi)
    dn = lax.dynamic_update_slice(dn, lax.dynamic_slice(dn, at, (width, width)) + own_ridge, at)

    bm = min(512, w)
    owner = (me_row == group) & (me_tm == tm_owner)
    low_block = offset // bm
    info = jnp.stack([
        jnp.where(owner, low_block, 0),
        jnp.where(owner, low_block + slab // bm, 0),
    ]).astype(jnp.int32)
    prior = None
    for c in range(chunks):
        prior = final_chunk(info, gathered[c], weights, d0, d1, dn, prior, c, chunks, cols, local, width, bm)
    return tuple(prior)


def solution(mesh):
    in_specs = (P("row", None, "tm", "col"), P(), P("col"), P(), P())
    out_specs = (P(("row", "tm"), "col"), P(None, ("row", "tm"), None))
    return jax.shard_map(
        on_device, mesh=mesh, in_specs=in_specs, out_specs=out_specs, check_vma=False
    )
```
